32 devices in a mesh: fsdp: 32 (over z, y, x, core).
Axes of the slice: x: 2, y: 2, z: 4, core: 2. Of those that a mesh axis runs over, the one named last changes fastest.
Arguments:
- layer_input: bfloat16 [8192, 1024], P('fsdp'), may hold values from -6 to 6
- cotangent: float32 [8192, 1024], P('fsdp'), may hold values from -6 to 6
- slot_seq: int32 [8192], P('fsdp'), may hold values from -1 to 8191, as said below
- slot_pos: int32 [8192], P('fsdp'), may hold values from 0 to 255, as said below
- w_query: bfloat16 [1024, 1024], P('fsdp'), may hold values from -0.1875 to 0.1875
- w_key: bfloat16 [1024, 1024], P('fsdp'), may hold values from -0.1875 to 0.1875
- w_value: bfloat16 [1024, 1024], P('fsdp'), may hold values from -0.1875 to 0.1875
- w_out: bfloat16 [1024, 1024], P('fsdp'), may hold values from -0.1875 to 0.1875
- query_gain: bfloat16 [1024], P('fsdp'), may hold values from 0.6 to 6
- key_gain: bfloat16 [1024], P('fsdp'), may hold values from 0.6 to 6
- attn_gain: bfloat16 [1024], P('fsdp'), may hold values from 0.099609375 to 1.8984375
- w_gate: bfloat16 [1024, 4096], P('fsdp'), may hold values from -0.1875 to 0.1875
- w_up: bfloat16 [1024, 4096], P('fsdp'), may hold values from -0.1875 to 0.1875
- w_down: bfloat16 [4096, 1024], P('fsdp'), may hold values from -0.09375 to 0.09375
- mlp_gain: bfloat16 [1024], P('fsdp'), may hold values from 0.099609375 to 1.8984375
Outputs:
- output: float32 [8192, 1024], P('fsdp')
- input_grad: float32 [8192, 1024], P('fsdp')
- grad_query: float32 [1024, 1024], P('fsdp')
- grad_key: float32 [1024, 1024], P('fsdp')
- grad_value: float32 [1024, 1024], P('fsdp')
- grad_out: float32 [1024, 1024], P('fsdp')
- grad_query_gain: float32 [1024], P('fsdp')
- grad_key_gain: float32 [1024], P('fsdp')
- grad_attn_gain: float32 [1024], P('fsdp')
- grad_gate: float32 [1024, 4096], P('fsdp')
- grad_up: float32 [1024, 4096], P('fsdp')
- grad_down: float32 [4096, 1024], P('fsdp')
- grad_mlp_gain: float32 [1024], P('fsdp')
The draws below stay inside these ranges and needn't reach their ends.
Inputs may be any that keep to these rules, and one draw needn't show every extreme that they name: `slot_seq`: each device's 256 slots hold whole sequences one after another from its first slot, then empty slots marked -1; a sequence's number is the index, in the whole array, of its last slot, so numbers rise from slot to slot; no sequence is longer than 256 slots and one is exactly 256; every device fills at least 102 slots and some device fills all. `slot_pos`: positions run 0, 1, 2 and so on through each sequence; empty slots hold 0.
All inputs are finite; a program needn't handle non-finite values.
Results may differ from the reference program's by a relative error of at most 0.015.
The reference program's roundings to bfloat16 on the way count: a program that leaves them out, or rounds other values in their place, can miss the bound.
Values may be sent and summed in bfloat16 or wider, within the bound.
No kernel may reach another device: no remote copies, remote signals or barrier semaphores. Data moves between devices by JAX's collectives and lax.ppermute only.
A program may use at most 192 MiB of HBM per device.

```python
import jax
import jax.numpy as jnp
from jax import lax

D = 1024
HEADS = 8
HEAD_DIM = 128
FF = 4096
TOK_DEV = 256
MAXLEN = 256
TOKENS = 8192
N_FSDP = 32


def slot_layout(key):
    key_fill, key_start = jax.random.split(jax.random.fold_in(key, 5), 2)
    local = jnp.arange(TOK_DEV, dtype=jnp.int32)
    devices = jnp.arange(N_FSDP, dtype=jnp.int32)
    fills = jax.random.randint(key_fill, (N_FSDP,), 2 * TOK_DEV // 5, TOK_DEV + 1)
    full_device = N_FSDP - 1
    fills = jnp.where(devices == full_device, TOK_DEV, fills)
    starts = jax.random.randint(key_start, (N_FSDP, TOK_DEV), 0, 48) == 0
    starts = starts | (local % MAXLEN == 0)[None, :]
    long_run = (devices == full_device)[:, None] & (local > 0)[None, :] & (local < MAXLEN)[None, :]
    starts = starts & jnp.logical_not(long_run)
    live = local[None, :] < fills[:, None]
    starts = starts & live
    next_start = jnp.concatenate([starts[:, 1:], jnp.ones((N_FSDP, 1), dtype=bool)], axis=1)
    next_live = jnp.concatenate([live[:, 1:], jnp.zeros((N_FSDP, 1), dtype=bool)], axis=1)
    ends = live & (next_start | jnp.logical_not(next_live))
    global_index = devices[:, None] * TOK_DEV + local[None, :]
    last_index = lax.cummin(jnp.where(ends, global_index, TOK_DEV * N_FSDP), axis=1, reverse=True)
    seq_number = jnp.where(live, last_index, -1)
    last_start = lax.cummax(jnp.where(starts, local[None, :], 0), axis=1)
    position = jnp.where(live, local[None, :] - last_start, 0)
    return (seq_number.reshape(-1).astype(jnp.int32), position.reshape(-1).astype(jnp.int32))


def draw_slot_seq(key, part):
    return slot_layout(key)[0]


def draw_slot_pos(key, part):
    return slot_layout(key)[1]


def gain_values(key):
    values = jax.random.uniform(key, (D,), jnp.float32, 0.6, 1.6)
    return values.astype(jnp.bfloat16)


def draw_query_gain(key, part):
    return gain_values(jax.random.fold_in(key, 11))


def draw_key_gain(key, part):
    return gain_values(jax.random.fold_in(key, 12))


def shard_levels(own_key, extent, cuts, least, top_value):
    gain = 1.0
    for dim, parts in cuts:
        draws = jax.random.uniform(jax.random.fold_in(jax.random.fold_in(own_key, 6), dim), (parts,), jnp.float32, least / len(cuts), top_value / len(cuts))
        gain = gain * jnp.repeat(jnp.exp(draws), extent[dim] // parts).reshape((-1,) + (1,) * (len(extent) - 1 - dim))
    return gain


def scatter_about(stream_key, shape, width, bound, shards=(), kind=jnp.bfloat16):
    values = jax.random.normal(stream_key, shape, jnp.float32) * width
    if len(shards) > 0:
        values = shard_levels(stream_key, shape, shards, -0.22, 0.18) * values
    return jnp.clip(values, min=-bound, max=bound).astype(kind)


def setup_inputs(seed: int = 0) -> dict:
    key_list = jax.random.split(jax.random.key(seed), 16)
    layer_input = scatter_about(key_list[0], (TOKENS, D), 1.0, 6.0, ((0, 32),))
    cotangent = scatter_about(key_list[1], (TOKENS, D), 1.0, 6.0, ((0, 32),), jnp.float32)
    slot_seq = draw_slot_seq(jax.random.fold_in(key_list[15], 71), 0)
    slot_pos = draw_slot_pos(jax.random.fold_in(key_list[15], 71), 0)
    w_query = scatter_about(key_list[4], (D, D), D ** -0.5, 0.1875, ((0, 32),))
    w_key = scatter_about(key_list[5], (D, D), D ** -0.5, 0.1875, ((0, 32),))
    w_value = scatter_about(key_list[6], (D, D), D ** -0.5, 0.1875, ((0, 32),))
    w_out = scatter_about(key_list[7], (D, D), D ** -0.5, 0.1875, ((0, 32),))
    query_gain = draw_query_gain(jax.random.fold_in(key_list[15], 71), 0)
    key_gain = draw_key_gain(jax.random.fold_in(key_list[15], 71), 0)
    attn_gain = jnp.clip(1.0 + 0.18 * jax.random.normal(key_list[10], (D,), jnp.float32), 0.099609375, 1.8984375).astype(jnp.bfloat16)
    w_gate = scatter_about(key_list[11], (D, FF), D ** -0.5, 0.1875, ((0, 32),))
    w_up = scatter_about(key_list[12], (D, FF), D ** -0.5, 0.1875, ((0, 32),))
    w_down = scatter_about(key_list[13], (FF, D), FF ** -0.5, 0.09375, ((0, 32),))
    mlp_gain = jnp.clip(1.0 + 0.18 * jax.random.normal(key_list[14], (D,), jnp.float32), 0.099609375, 1.8984375).astype(jnp.bfloat16)
    return {"layer_input": layer_input, "cotangent": cotangent, "slot_seq": slot_seq, "slot_pos": slot_pos, "w_query": w_query, "w_key": w_key, "w_value": w_value, "w_out": w_out, "query_gain": query_gain, "key_gain": key_gain, "attn_gain": attn_gain, "w_gate": w_gate, "w_up": w_up, "w_down": w_down, "mlp_gain": mlp_gain}


epsilon = 1e-06
rope_base = 500000.0

def inverse_rms(values):
    return lax.rsqrt(lax.optimization_barrier(jnp.mean(values * values, axis=-1, keepdims=True)) + epsilon)

def norm_back(grad_hat, hat_values, inverse):
    return inverse * (grad_hat - hat_values * lax.optimization_barrier(jnp.mean(grad_hat * hat_values, axis=-1, keepdims=True)))

def rope_tables(positions):
    half = HEAD_DIM // 2
    freq = rope_base ** (-(jnp.arange(half, dtype=jnp.float32) * 2.0 / HEAD_DIM))
    angle = positions.astype(jnp.float32)[:, None] * freq[None, :]
    return (jnp.cos(angle)[:, None, :], jnp.sin(angle)[:, None, :])

def rope_apply(values, cosine, sine):
    half = values.shape[-1] // 2
    first = values[..., :half]
    second = values[..., half:]
    return jnp.concatenate([first * cosine - second * sine, second * cosine + first * sine], axis=-1)

def rope_back(grads, cosine, sine):
    half = grads.shape[-1] // 2
    first = grads[..., :half]
    second = grads[..., half:]
    return jnp.concatenate([first * cosine + second * sine, second * cosine - first * sine], axis=-1)

def masked_scores(query_rot, key_rot, seq_ids, positions):
    scores = jnp.einsum('qhd,khd->hqk', query_rot.astype(jnp.float32), key_rot.astype(jnp.float32)) * HEAD_DIM ** (-0.5)
    allowed = (seq_ids[:, None] == seq_ids[None, :]) & (positions[None, :] <= positions[:, None])
    return jnp.where(allowed[None], scores, -jnp.inf)

def left_product(first, second):
    return jnp.dot(first.T, second, preferred_element_type=jnp.float32)

def right_product(first, second):
    return jnp.dot(first, second.T, preferred_element_type=jnp.float32)

def block_pass(tokens, cotangent_rows, seq_ids, positions, weights):
    w_query, w_key, w_value, w_out, query_gain, key_gain, attn_gain, w_gate, w_up, w_down, mlp_gain = weights
    rows = tokens.shape[0]
    live = (seq_ids >= 0).astype(jnp.float32)[:, None]
    query = jnp.dot(tokens, w_query, preferred_element_type=jnp.float32)
    keys_raw = jnp.dot(tokens, w_key, preferred_element_type=jnp.float32)
    values_raw = jnp.dot(tokens, w_value, preferred_element_type=jnp.float32)
    query_inv = inverse_rms(query)
    query_hat = query * query_inv
    key_inv = inverse_rms(keys_raw)
    key_hat = keys_raw * key_inv
    cosine, sine = rope_tables(positions)
    query_rot = rope_apply((query_hat * query_gain.astype(jnp.float32)).reshape(rows, HEADS, HEAD_DIM), cosine, sine).astype(jnp.bfloat16)
    key_rot = rope_apply((key_hat * key_gain.astype(jnp.float32)).reshape(rows, HEADS, HEAD_DIM), cosine, sine).astype(jnp.bfloat16)
    value_b = values_raw.astype(jnp.bfloat16).reshape(rows, HEADS, HEAD_DIM)
    scores = masked_scores(query_rot, key_rot, seq_ids, positions)
    peak = lax.optimization_barrier(jnp.max(scores, axis=-1, keepdims=True))
    log_total = peak + jnp.log(lax.optimization_barrier(jnp.sum(jnp.exp(scores - peak), axis=-1, keepdims=True)))
    probs = jnp.exp(scores - log_total)
    probs_b = probs.astype(jnp.bfloat16)
    heads_out = jnp.einsum('hqk,khd->qhd', probs_b.astype(jnp.float32), value_b.astype(jnp.float32)).reshape(rows, D).astype(jnp.bfloat16)
    attn_proj = jnp.dot(heads_out, w_out, preferred_element_type=jnp.float32)
    attn_inv = inverse_rms(attn_proj)
    attn_hat = attn_proj * attn_inv
    hidden_state = tokens.astype(jnp.float32) + attn_hat * attn_gain.astype(jnp.float32)
    hidden_b = hidden_state.astype(jnp.bfloat16)
    gate_pre = jnp.dot(hidden_b, w_gate, preferred_element_type=jnp.float32)
    up_pre = jnp.dot(hidden_b, w_up, preferred_element_type=jnp.float32)
    sigma = jax.nn.sigmoid(gate_pre)
    activated = gate_pre * sigma
    mixed_b = (activated * up_pre).astype(jnp.bfloat16)
    ffn_out = jnp.dot(mixed_b, w_down, preferred_element_type=jnp.float32)
    ffn_inv = inverse_rms(ffn_out)
    ffn_hat = ffn_out * ffn_inv
    output = (hidden_state + ffn_hat * mlp_gain.astype(jnp.float32)) * live
    upstream = cotangent_rows * live
    grad_mlp_gain = lax.optimization_barrier(jnp.sum(upstream * ffn_hat, axis=0))
    ffn_grad_b = norm_back(upstream * mlp_gain.astype(jnp.float32), ffn_hat, ffn_inv).astype(jnp.bfloat16)
    grad_down = left_product(mixed_b, ffn_grad_b)
    mixed_grad = right_product(ffn_grad_b, w_down)
    gate_grad_b = (mixed_grad * up_pre * sigma * (1.0 + gate_pre * (1.0 - sigma))).astype(jnp.bfloat16)
    up_grad_b = (mixed_grad * activated).astype(jnp.bfloat16)
    grad_gate = left_product(hidden_b, gate_grad_b)
    grad_up = left_product(hidden_b, up_grad_b)
    hidden_grad = upstream + right_product(gate_grad_b, w_gate) + right_product(up_grad_b, w_up)
    grad_attn_gain = lax.optimization_barrier(jnp.sum(hidden_grad * attn_hat, axis=0))
    attn_grad_b = norm_back(hidden_grad * attn_gain.astype(jnp.float32), attn_hat, attn_inv).astype(jnp.bfloat16)
    grad_out = left_product(heads_out, attn_grad_b)
    heads_grad_b = right_product(attn_grad_b, w_out).astype(jnp.bfloat16).reshape(rows, HEADS, HEAD_DIM)
    scores_again = masked_scores(query_rot, key_rot, seq_ids, positions)
    probs_again = jnp.exp(scores_again - log_total)
    probs_again_b = probs_again.astype(jnp.bfloat16)
    prob_grad = jnp.einsum('qhd,khd->hqk', heads_grad_b.astype(jnp.float32), value_b.astype(jnp.float32))
    row_dot = lax.optimization_barrier(jnp.sum(probs_again * prob_grad, axis=-1, keepdims=True))
    score_grad_b = (probs_again * (prob_grad - row_dot) * HEAD_DIM ** (-0.5)).astype(jnp.bfloat16)
    query_rot_grad = jnp.einsum('hqk,khd->qhd', score_grad_b.astype(jnp.float32), key_rot.astype(jnp.float32))
    key_rot_grad = jnp.einsum('hqk,qhd->khd', score_grad_b.astype(jnp.float32), query_rot.astype(jnp.float32))
    value_grad_b = jnp.einsum('hqk,qhd->khd', probs_again_b.astype(jnp.float32), heads_grad_b.astype(jnp.float32)).reshape(rows, D).astype(jnp.bfloat16)
    query_norm_grad = rope_back(query_rot_grad, cosine, sine).reshape(rows, D)
    key_norm_grad = rope_back(key_rot_grad, cosine, sine).reshape(rows, D)
    grad_query_gain = lax.optimization_barrier(jnp.sum(query_norm_grad * query_hat, axis=0))
    grad_key_gain = lax.optimization_barrier(jnp.sum(key_norm_grad * key_hat, axis=0))
    query_grad_b = norm_back(query_norm_grad * query_gain.astype(jnp.float32), query_hat, query_inv).astype(jnp.bfloat16)
    key_grad_b = norm_back(key_norm_grad * key_gain.astype(jnp.float32), key_hat, key_inv).astype(jnp.bfloat16)
    grad_query = left_product(tokens, query_grad_b)
    grad_key = left_product(tokens, key_grad_b)
    grad_value = left_product(tokens, value_grad_b)
    input_grad = hidden_grad + right_product(query_grad_b, w_query) + right_product(key_grad_b, w_key) + right_product(value_grad_b, w_value)
    grads = (grad_query, grad_key, grad_value, grad_out, grad_query_gain, grad_key_gain, grad_attn_gain, grad_gate, grad_up, grad_down, grad_mlp_gain)
    return (output, input_grad, grads)

def reference(layer_input, cotangent, slot_seq, slot_pos, w_query, w_key, w_value, w_out, query_gain, key_gain, attn_gain, w_gate, w_up, w_down, mlp_gain):
    weights = (w_query, w_key, w_value, w_out, query_gain, key_gain, attn_gain, w_gate, w_up, w_down, mlp_gain)
    shapes = [(D, D), (D, D), (D, D), (D, D), (D,), (D,), (D,), (D, FF), (D, FF), (FF, D), (D,)]
    zeros = tuple((jnp.zeros(shape, jnp.float32) for shape in shapes))
    stacked = (layer_input.reshape(N_FSDP, TOK_DEV, D), cotangent.reshape(N_FSDP, TOK_DEV, D), slot_seq.reshape(N_FSDP, TOK_DEV), slot_pos.reshape(N_FSDP, TOK_DEV))

    def step(carry, item):
        output, input_grad, grads = block_pass(item[0], item[1], item[2], item[3], weights)
        return (tuple((total + term for total, term in zip(carry, grads))), (output, input_grad))
    totals, (outputs, input_grads) = lax.scan(step, zeros, stacked)
    return (outputs.reshape(TOKENS, D), input_grads.reshape(TOKENS, D), totals[0], totals[1], totals[2], totals[3], totals[4], totals[5], totals[6], totals[7], totals[8], totals[9], totals[10])
```

```python
import functools

import jax
import jax.numpy as jnp
from jax import lax
from jax.experimental import pallas as pl
from jax.experimental.pallas import tpu as pltpu
from jax.sharding import PartitionSpec as P

HEADS = 8
HEAD_DIM = 128


epsilon = 1e-06
rope_base = 500000.0


def inverse_rms(values):
    return lax.rsqrt(jnp.mean(values * values, axis=-1, keepdims=True) + epsilon)


def norm_back(grad_hat, hat_values, inverse):
    return inverse * (
        grad_hat - hat_values * jnp.mean(grad_hat * hat_values, axis=-1, keepdims=True)
    )


def rope_tables(positions):
    half = HEAD_DIM // 2
    freq = rope_base ** (-(jnp.arange(half, dtype=jnp.float32) * 2.0 / HEAD_DIM))
    angle = positions.astype(jnp.float32)[:, None] * freq[None, :]
    return (jnp.cos(angle)[:, None, :], jnp.sin(angle)[:, None, :])


def rope_apply(values, cosine, sine):
    half = values.shape[-1] // 2
    first = values[..., :half]
    second = values[..., half:]
    return jnp.concatenate(
        [first * cosine - second * sine, second * cosine + first * sine], axis=-1
    )


def rope_back(grads, cosine, sine):
    half = grads.shape[-1] // 2
    first = grads[..., :half]
    second = grads[..., half:]
    return jnp.concatenate(
        [first * cosine + second * sine, second * cosine - first * sine], axis=-1
    )


def masked_scores(query_rot, key_rot, seq_ids, positions):
    scores = jnp.einsum(
        "qhd,khd->hqk", query_rot, key_rot, preferred_element_type=jnp.float32
    ) * HEAD_DIM ** (-0.5)
    allowed = (seq_ids[:, None] == seq_ids[None, :]) & (positions[None, :] <= positions[:, None])
    return jnp.where(allowed[None], scores, -jnp.inf)


def left_product(first, second):
    return lax.dot_general(
        first, second, (((0,), (0,)), ((), ())), preferred_element_type=jnp.float32
    )


def right_product(first, second):
    return lax.dot_general(
        first, second, (((1,), (1,)), ((), ())), preferred_element_type=jnp.float32
    )


def dot_nn(first, second):
    return lax.dot_general(
        first, second, (((1,), (0,)), ((), ())), preferred_element_type=jnp.float32
    )


def ffn_kernel(
    hidden_ref,
    cot_ref,
    live_ref,
    gain_ref,
    gate_ref,
    up_ref,
    down_ref,
    output_ref,
    hidden_grad_ref,
    gain_grad_ref,
    grads_ref,
    hidden_b_ref,
    gate_pre_ref,
    up_pre_ref,
    mixed_ref,
    ffn_out_ref,
    ffn_grad_ref,
    gate_out_ref,
    up_out_ref,
    down_out_ref,
    sems,
    *,
    blocks,
    unit,
):
    phase = pl.program_id(0)
    step = pl.program_id(1)
    width = hidden_ref.shape[1]
    inner, outer = grads_ref.shape[0], grads_ref.shape[1]

    @pl.when(phase == 0)
    def forward():
        @pl.when(step == 0)
        def start():
            hidden_b_ref[...] = hidden_ref[...].astype(jnp.bfloat16)
            ffn_out_ref[...] = jnp.zeros_like(ffn_out_ref)

        hidden_b = hidden_b_ref[...]
        gate_pre = dot_nn(hidden_b, gate_ref[...].reshape(width, width))
        up_pre = dot_nn(hidden_b, up_ref[...].reshape(width, width))
        gate_pre_ref[step] = gate_pre
        up_pre_ref[step] = up_pre
        mixed_b = (gate_pre * jax.nn.sigmoid(gate_pre) * up_pre).astype(jnp.bfloat16)
        mixed_ref[step] = mixed_b
        ffn_out_ref[...] += dot_nn(mixed_b, down_ref[...].reshape(width, width))

        @pl.when(step == blocks - 1)
        def finish():
            live = live_ref[...]
            gain = gain_ref[...]
            ffn_out = ffn_out_ref[...]
            ffn_inv = inverse_rms(ffn_out)
            ffn_hat = ffn_out * ffn_inv
            output_ref[...] = (hidden_ref[...] + ffn_hat * gain) * live
            upstream = cot_ref[...] * live
            gain_grad_ref[...] = jnp.sum(upstream * ffn_hat, axis=0, keepdims=True)
            ffn_grad_ref[...] = norm_back(upstream * gain, ffn_hat, ffn_inv).astype(jnp.bfloat16)
            hidden_grad_ref[...] = upstream

    @pl.when(phase == 1)
    def backward():
        block = blocks - 1 - step
        gate_copy = pltpu.make_async_copy(
            gate_out_ref, grads_ref.at[:, :, pl.ds((blocks + block) * unit, unit)], sems.at[0]
        )
        up_copy = pltpu.make_async_copy(
            up_out_ref, grads_ref.at[:, :, pl.ds((2 * blocks + block) * unit, unit)], sems.at[1]
        )
        down_copy = pltpu.make_async_copy(
            down_out_ref, grads_ref.at[:, block, pl.ds(0, blocks * unit)], sems.at[2]
        )
        ffn_grad_b = ffn_grad_ref[...]
        hidden_b = hidden_b_ref[...]
        gate_pre = gate_pre_ref[block]
        up_pre = up_pre_ref[block]
        mixed_grad = right_product(ffn_grad_b, down_ref[...].reshape(width, width))
        sigma = jax.nn.sigmoid(gate_pre)
        gate_grad_b = (mixed_grad * up_pre * sigma * (1.0 + gate_pre * (1.0 - sigma))).astype(
            jnp.bfloat16
        )
        up_grad_b = (mixed_grad * (gate_pre * sigma)).astype(jnp.bfloat16)
        hidden_grad_ref[...] += right_product(
            gate_grad_b, gate_ref[...].reshape(width, width)
        ) + right_product(up_grad_b, up_ref[...].reshape(width, width))
        grad_down = left_product(mixed_ref[block], ffn_grad_b).astype(jnp.bfloat16)

        @pl.when(step > 0)
        def drain():
            gate_copy.wait()
            up_copy.wait()
            down_copy.wait()

        down_out_ref[...] = grad_down.reshape(inner, blocks * unit, width)
        down_copy.start()
        grad_gate = left_product(hidden_b, gate_grad_b).astype(jnp.bfloat16)
        grad_gate = grad_gate.reshape(outer, inner, unit, width)
        for plane in range(outer):
            gate_out_ref[:, plane] = grad_gate[plane]
        gate_copy.start()
        grad_up = left_product(hidden_b, up_grad_b).astype(jnp.bfloat16)
        grad_up = grad_up.reshape(outer, inner, unit, width)
        for plane in range(outer):
            up_out_ref[:, plane] = grad_up[plane]
        up_copy.start()

        @pl.when(step == blocks - 1)
        def finish():
            gate_copy.wait()
            up_copy.wait()
            down_copy.wait()


def ffn(hidden_state, cotangent, live, gain, gathered, blocks, unit, outer):
    rows, width = hidden_state.shape
    devices = gathered.shape[0]
    inner = devices // outer
    grad_rows = 3 * blocks * unit
    whole = lambda phase, step: (0, 0)
    order = lambda phase, step: phase * (blocks - 1 - step) + (1 - phase) * step
    first_gate = blocks + 4
    first_up = first_gate + blocks
    return pl.pallas_call(
        lambda *refs: ffn_kernel(*refs, blocks=blocks, unit=unit),
        grid=(2, blocks),
        in_specs=[
            pl.BlockSpec((rows, width), whole),
            pl.BlockSpec((rows, width), whole),
            pl.BlockSpec((rows, 1), whole),
            pl.BlockSpec((1, width), whole),
            pl.BlockSpec((devices, unit, width), lambda p, s: (0, first_gate + order(p, s), 0)),
            pl.BlockSpec((devices, unit, width), lambda p, s: (0, first_up + order(p, s), 0)),
            pl.BlockSpec(
                (devices // blocks, blocks * unit, width), lambda p, s: (order(p, s), 0, 0)
            ),
        ],
        out_specs=[
            pl.BlockSpec((rows, width), whole),
            pl.BlockSpec((rows, width), whole),
            pl.BlockSpec((1, width), whole),
            pl.BlockSpec(memory_space=pl.ANY),
        ],
        out_shape=[
            jax.ShapeDtypeStruct((rows, width), jnp.float32),
            jax.ShapeDtypeStruct((rows, width), jnp.float32),
            jax.ShapeDtypeStruct((1, width), jnp.float32),
            jax.ShapeDtypeStruct((inner, outer, grad_rows, width), jnp.bfloat16),
        ],
        scratch_shapes=[
            pltpu.VMEM((rows, width), jnp.bfloat16),
            pltpu.VMEM((blocks, rows, width), jnp.float32),
            pltpu.VMEM((blocks, rows, width), jnp.float32),
            pltpu.VMEM((blocks, rows, width), jnp.bfloat16),
            pltpu.VMEM((rows, width), jnp.float32),
            pltpu.VMEM((rows, width), jnp.bfloat16),
            pltpu.VMEM((inner, outer, unit, width), jnp.bfloat16),
            pltpu.VMEM((inner, outer, unit, width), jnp.bfloat16),
            pltpu.VMEM((inner, blocks * unit, width), jnp.bfloat16),
            pltpu.SemaphoreType.DMA((3,)),
        ],
        compiler_params=pltpu.CompilerParams(
            dimension_semantics=("arbitrary", "arbitrary"), vmem_limit_bytes=60 << 20
        ),
    )(hidden_state, cotangent, live, gain, gathered, gathered, gathered)


def local(
    devices,
    layer_input,
    cotangent,
    slot_seq,
    slot_pos,
    w_query,
    w_key,
    w_value,
    w_out,
    query_gain,
    key_gain,
    attn_gain,
    w_gate,
    w_up,
    w_down,
    mlp_gain,
):
    rows = layer_input.shape[0]
    width = layer_input.shape[1]
    unit = w_query.shape[0]
    hidden_units = w_gate.shape[1]
    blocks = hidden_units // width
    outer = blocks
    inner = devices // outer
    planes = [[plane * inner + spot for spot in range(inner)] for plane in range(outer)]
    columns = [[plane * inner + spot for plane in range(outer)] for spot in range(inner)]
    live = (slot_seq >= 0).astype(jnp.float32)[:, None]

    def by_block(weight):
        return weight.reshape(unit, blocks, width).transpose(1, 0, 2).reshape(blocks * unit, width)

    gains = jnp.concatenate([query_gain, key_gain, attn_gain, mlp_gain])
    gains = jnp.pad(gains[None, :], ((0, 7), (0, width - 4 * unit)))
    packed = jnp.concatenate(
        [w_down, w_query, w_key, w_value, w_out, by_block(w_gate), by_block(w_up), gains], axis=0
    )
    gathered = lax.all_gather(packed, "fsdp", axis=0, tiled=False)

    def square(index):
        start = (blocks + index) * unit
        return gathered[:, start : start + unit].reshape(width, width)

    full_query, full_key, full_value, full_out = (square(index) for index in range(4))
    gain_row = (3 * blocks + 4) * unit
    all_gains = gathered[:, gain_row, : 4 * unit].astype(jnp.float32)
    gain_query, gain_key, gain_attn, gain_mlp = (
        all_gains[:, index * unit : (index + 1) * unit].reshape(width) for index in range(4)
    )
    query = jnp.dot(layer_input, full_query, preferred_element_type=jnp.float32)
    keys_raw = jnp.dot(layer_input, full_key, preferred_element_type=jnp.float32)
    values_raw = jnp.dot(layer_input, full_value, preferred_element_type=jnp.float32)
    query_inv = inverse_rms(query)
    query_hat = query * query_inv
    key_inv = inverse_rms(keys_raw)
    key_hat = keys_raw * key_inv
    cosine, sine = rope_tables(slot_pos)
    query_rot = rope_apply(
        (query_hat * gain_query).reshape(rows, HEADS, HEAD_DIM), cosine, sine
    ).astype(jnp.bfloat16)
    key_rot = rope_apply(
        (key_hat * gain_key).reshape(rows, HEADS, HEAD_DIM), cosine, sine
    ).astype(jnp.bfloat16)
    value_b = values_raw.astype(jnp.bfloat16).reshape(rows, HEADS, HEAD_DIM)
    scores = masked_scores(query_rot, key_rot, slot_seq, slot_pos)
    peak = jnp.max(scores, axis=-1, keepdims=True)
    log_total = peak + jnp.log(jnp.sum(jnp.exp(scores - peak), axis=-1, keepdims=True))
    probs_b = jnp.exp(scores - log_total).astype(jnp.bfloat16)
    heads_out = (
        jnp.einsum("hqk,khd->qhd", probs_b, value_b, preferred_element_type=jnp.float32)
        .reshape(rows, width)
        .astype(jnp.bfloat16)
    )
    attn_proj = jnp.dot(heads_out, full_out, preferred_element_type=jnp.float32)
    attn_inv = inverse_rms(attn_proj)
    attn_hat = attn_proj * attn_inv
    hidden_state = layer_input.astype(jnp.float32) + attn_hat * gain_attn
    output, hidden_grad, grad_mlp_gain, ffn_grads = ffn(
        hidden_state, cotangent, live, gain_mlp[None, :], gathered, blocks, unit, outer
    )
    ffn_part = lax.psum_scatter(
        ffn_grads, "fsdp", scatter_dimension=0, tiled=True, axis_index_groups=planes
    )
    grad_attn_gain = jnp.sum(hidden_grad * attn_hat, axis=0)
    attn_grad_b = norm_back(hidden_grad * gain_attn, attn_hat, attn_inv).astype(jnp.bfloat16)
    grad_out_weight = left_product(heads_out, attn_grad_b)
    heads_grad_b = (
        right_product(attn_grad_b, full_out).astype(jnp.bfloat16).reshape(rows, HEADS, HEAD_DIM)
    )
    scores_again = masked_scores(query_rot, key_rot, slot_seq, slot_pos)
    probs_again = jnp.exp(scores_again - log_total)
    probs_again_b = probs_again.astype(jnp.bfloat16)
    prob_grad = jnp.einsum(
        "qhd,khd->hqk", heads_grad_b, value_b, preferred_element_type=jnp.float32
    )
    row_dot = jnp.sum(probs_again * prob_grad, axis=-1, keepdims=True)
    score_grad_b = (probs_again * (prob_grad - row_dot) * HEAD_DIM ** (-0.5)).astype(jnp.bfloat16)
    query_rot_grad = jnp.einsum(
        "hqk,khd->qhd", score_grad_b, key_rot, preferred_element_type=jnp.float32
    )
    key_rot_grad = jnp.einsum(
        "hqk,qhd->khd", score_grad_b, query_rot, preferred_element_type=jnp.float32
    )
    value_grad_b = (
        jnp.einsum("hqk,qhd->khd", probs_again_b, heads_grad_b, preferred_element_type=jnp.float32)
        .reshape(rows, width)
        .astype(jnp.bfloat16)
    )
    query_norm_grad = rope_back(query_rot_grad, cosine, sine).reshape(rows, width)
    key_norm_grad = rope_back(key_rot_grad, cosine, sine).reshape(rows, width)
    grad_query_gain = jnp.sum(query_norm_grad * query_hat, axis=0)
    grad_key_gain = jnp.sum(key_norm_grad * key_hat, axis=0)
    query_grad_b = norm_back(query_norm_grad * gain_query, query_hat, query_inv).astype(
        jnp.bfloat16
    )
    key_grad_b = norm_back(key_norm_grad * gain_key, key_hat, key_inv).astype(jnp.bfloat16)
    grad_query_weight = left_product(layer_input, query_grad_b)
    grad_key_weight = left_product(layer_input, key_grad_b)
    grad_value_weight = left_product(layer_input, value_grad_b)

    def to_owners(weight):
        return weight.astype(jnp.bfloat16).reshape(outer, inner, unit, width).transpose(1, 0, 2, 3)

    gain_grads = jnp.stack([grad_query_gain, grad_key_gain, grad_attn_gain, grad_mlp_gain[0]])
    gain_grads = gain_grads.reshape(4, outer, inner, unit).transpose(2, 1, 0, 3)
    gain_grads = gain_grads.reshape(inner, outer, 1, 4 * unit).astype(jnp.bfloat16)
    gain_grads = jnp.pad(gain_grads, ((0, 0), (0, 0), (0, 7), (0, width - 4 * unit)))
    attn_grads = jnp.concatenate(
        [
            to_owners(grad_query_weight),
            to_owners(grad_key_weight),
            to_owners(grad_value_weight),
            to_owners(grad_out_weight),
            gain_grads,
        ],
        axis=2,
    )
    attn_part = lax.psum_scatter(
        attn_grads, "fsdp", scatter_dimension=0, tiled=True, axis_index_groups=planes
    )
    both = jnp.concatenate([ffn_part[0], attn_part[0]], axis=1)
    owned = lax.psum_scatter(
        both, "fsdp", scatter_dimension=0, tiled=True, axis_index_groups=columns
    )[0]
    input_grad = (
        hidden_grad
        + right_product(query_grad_b, full_query)
        + right_product(key_grad_b, full_key)
        + right_product(value_grad_b, full_value)
    )
    owned = owned.astype(jnp.float32)

    def section(start, count):
        return owned[start * unit : (start + count) * unit]

    def from_blocks(part):
        return part.reshape(blocks, unit, width).transpose(1, 0, 2).reshape(unit, hidden_units)

    first = 3 * blocks
    gain_out = owned[(first + 4) * unit, : 4 * unit]
    return (
        output,
        input_grad,
        section(first, 1),
        section(first + 1, 1),
        section(first + 2, 1),
        section(first + 3, 1),
        gain_out[:unit],
        gain_out[unit : 2 * unit],
        gain_out[2 * unit : 3 * unit],
        from_blocks(section(blocks, blocks)),
        from_blocks(section(2 * blocks, blocks)),
        section(0, blocks),
        gain_out[3 * unit :],
    )


def solution(mesh):
    return jax.shard_map(
        functools.partial(local, mesh.shape["fsdp"]),
        mesh=mesh,
        in_specs=(
            P("fsdp", None),
            P("fsdp", None),
            P("fsdp"),
            P("fsdp"),
            P("fsdp", None),
            P("fsdp", None),
            P("fsdp", None),
            P("fsdp", None),
            P("fsdp"),
            P("fsdp"),
            P("fsdp"),
            P("fsdp", None),
            P("fsdp", None),
            P("fsdp", None),
            P("fsdp"),
        ),
        out_specs=(
            P("fsdp", None),
            P("fsdp", None),
            P("fsdp", None),
            P("fsdp", None),
            P("fsdp", None),
            P("fsdp", None),
            P("fsdp"),
            P("fsdp"),
            P("fsdp"),
            P("fsdp", None),
            P("fsdp", None),
            P("fsdp", None),
            P("fsdp"),
        ),
        check_vma=False,
    )
```
